32 devices in a mesh: grp: 2 (over y), seq: 16 (over z, x, core).
Axes of the slice: x: 2, y: 2, z: 4, core: 2. Of those that a mesh axis runs over, the one named last changes fastest.
Arguments:
- queries: bfloat16 [192, 8, 4096], P('seq', 'grp'), parts along dimension 1, may hold values from -7 to 7
- keys: bfloat16 [192, 8, 4096], P('seq', 'grp'), parts along dimension 1, may hold values from -7 to 7
- values: bfloat16 [192, 8, 4096], P('seq', 'grp'), parts along dimension 1, may hold values from -6 to 6
- clip_frames: int32 [8], P('grp'), parts along dimension 0, may hold values from 1 to 8, as said below
Outputs:
- attended: bfloat16 [192, 8, 4096], P('seq', 'grp'), parts along dimension 1
The draws below stay inside these ranges and needn't reach their ends.
There are 2 independent parts, one for each index of `grp`. The reference program is written for one: setup_inputs(seed, part) draws one part's arguments, and reference() takes and returns one part's arrays. A program takes and returns all parts, laid end to end along the dimension named above; each array names one. Nothing has to cross between parts.
Inputs may be any that keep to these rules, and one draw needn't show every extreme that they name: Tokens of clip s at positions clip_frames[s] * 24 and later hold no data; some clip has all 8 frames.
All inputs are finite; a program needn't handle non-finite values.
Results may differ from the reference program's by a relative error of at most 0.0048.
Values may be sent and summed in bfloat16 or wider, within the bound.
A program may use at most 64 MiB of HBM per device.

```python
import math
import jax
import jax.numpy as jnp
from jax import lax

SEQS = 4
LENGTH = 192
HEADS = 32
HDIM = 128
HD = 4096
FRAMES = 8


def paired_fields(key):
    base_key = jax.random.fold_in(key, 17)
    query_key, key_key = jax.random.split(base_key, 2)
    field_shape = (LENGTH, SEQS, HEADS, HDIM)
    query_field = jnp.clip(1.8 * jax.random.normal(query_key, field_shape, jnp.float32), -7.0, 7.0)
    key_field = jnp.clip(1.8 * jax.random.normal(key_key, field_shape, jnp.float32), -7.0, 7.0)
    query_field = query_field.reshape(LENGTH, SEQS, HEADS * HDIM)
    key_field = key_field.reshape(LENGTH, SEQS, HEADS * HDIM)
    return (query_field, key_field)


def draw_queries(key, part):
    return paired_fields(key)[0].astype(jnp.bfloat16)


def draw_keys(key, part):
    return paired_fields(key)[1].astype(jnp.bfloat16)


def draw_clip_frames(key, part):
    base_key = jax.random.fold_in(key, 29)
    count_key, full_key = jax.random.split(base_key, 2)
    counts = jax.random.randint(count_key, (SEQS,), 1, FRAMES + 1)
    full_clip = jax.random.randint(full_key, (), 0, SEQS)
    return counts.at[full_clip].set(FRAMES).astype(jnp.int32)


def steps_of(key, shape, pieces, low, top_value):
    def one(dim, blocks):
        draws = jax.random.uniform(jax.random.fold_in(jax.random.fold_in(key, 6), dim), (blocks,), jnp.float32, low / len(pieces), top_value / len(pieces))
        return jnp.repeat(jnp.exp(draws), shape[dim] // blocks).reshape((-1,) + (1,) * (len(shape) - dim - 1))

    loudness = one(*pieces[0])
    for cut in pieces[1:]:
        loudness = loudness * one(*cut)
    return loudness


def scatter_about(stream_key, shape, deviation, limit, shards=(), kind=jnp.bfloat16):
    array = jax.random.normal(stream_key, shape, jnp.float32) * deviation
    if len(shards) > 0:
        array = steps_of(stream_key, shape, shards, -0.22, 0.18) * array
    return jnp.clip(array, min=-limit, max=limit).astype(kind)


def setup_inputs(seed: int = 0, part: int = 0) -> dict:
    streams_of = jax.random.split(jax.random.key(seed), 5)
    own_keys = jax.random.split(jax.random.fold_in(streams_of[4], part), 5)
    return {
        "queries": draw_queries(jax.random.fold_in(jax.random.fold_in(streams_of[4], part), 71), part),
        "keys": draw_keys(jax.random.fold_in(jax.random.fold_in(streams_of[4], part), 71), part),
        "values": scatter_about(own_keys[2], (LENGTH, SEQS, HD), 1.0, 6.0, ((0, 16),)),
        "clip_frames": draw_clip_frames(jax.random.fold_in(jax.random.fold_in(streams_of[4], part), 71), part),
    }


def reference(queries, keys, values, clip_frames):
    item_count = SEQS * HEADS
    score_scale = 1.0 / math.sqrt(HDIM)
    query_items = jnp.transpose(queries.reshape(LENGTH, item_count, HDIM), (1, 0, 2))
    key_items = jnp.transpose(keys.reshape(LENGTH, item_count, HDIM), (1, 0, 2))
    value_items = jnp.transpose(values.reshape(LENGTH, item_count, HDIM), (1, 0, 2))
    limits = jnp.repeat(clip_frames * (LENGTH // FRAMES), HEADS)
    positions = jnp.arange(LENGTH, dtype=jnp.int32)

    def attend_item(operands):
        query_rows, key_rows, value_rows, limit_value = operands
        scores = jnp.dot(query_rows, key_rows.T, preferred_element_type=jnp.float32) * score_scale
        scores = jnp.where(positions[None, :] < limit_value, scores, -jnp.inf)
        row_max = lax.optimization_barrier(jnp.max(scores, axis=1, keepdims=True))
        exponent = jnp.exp(scores - row_max)
        weights = (exponent / lax.optimization_barrier(jnp.sum(exponent, axis=1, keepdims=True))).astype(jnp.bfloat16)
        return jnp.dot(weights, value_rows, preferred_element_type=jnp.float32).astype(jnp.bfloat16)
    outputs = lax.map(attend_item, (query_items, key_items, value_items, limits))
    return jnp.transpose(outputs, (1, 0, 2)).reshape(LENGTH, SEQS, HEADS * HDIM)
```

```python
import functools
import math

import jax
import jax.numpy as jnp
from jax import lax
from jax.experimental import pallas as pl
from jax.experimental.pallas import tpu as pltpu
from jax.sharding import PartitionSpec as P

HEADS = 32
HDIM = 128
FRAMES = 8


neg_large = -1e30


def attend_block(query_block, key_rows, value_rows, key_bias):
    scores = jnp.einsum("qnd,knd->nqk", query_block, key_rows, preferred_element_type=jnp.float32)
    scores = scores * (1.0 / math.sqrt(HDIM)) + jnp.transpose(key_bias)[:, None, :]
    row_max = jnp.max(scores, axis=2, keepdims=True)
    exponent = jnp.exp(scores - row_max)
    weights = (exponent / jnp.sum(exponent, axis=2, keepdims=True)).astype(jnp.bfloat16)
    combined = jnp.einsum("nqk,knd->qnd", weights, value_rows, preferred_element_type=jnp.float32)
    return combined.astype(jnp.bfloat16)


def attend_all(query_rows, key_rows, value_rows, key_bias):
    length, item_count, head_dim = query_rows.shape
    block_rows = min(512, length)
    blocked = query_rows.reshape(length // block_rows, block_rows, item_count, head_dim)
    combined = lax.map(
        lambda query_block: attend_block(query_block, key_rows, value_rows, key_bias), blocked
    )
    return combined.reshape(length, item_count, head_dim)


def body(queries, keys, values, clip_frames):
    tokens, seq_count, feature_dim = queries.shape
    devices = lax.axis_size("seq")
    device_index = lax.axis_index("seq")
    slot_count = seq_count * HEADS
    per_device = slot_count // devices
    length = tokens * devices
    frame_tokens = length // FRAMES
    query_slots = queries.reshape(tokens, devices, per_device, HDIM)
    key_slots = keys.reshape(tokens, devices, per_device, HDIM)
    value_slots = values.reshape(tokens, devices, per_device, HDIM)
    slot_limit = jnp.repeat(clip_frames * frame_tokens, HEADS)
    query_all, key_all, value_all = (
        lax.all_to_all(query_slots, "seq", split_axis=1, concat_axis=0, tiled=True),
        lax.all_to_all(key_slots, "seq", split_axis=1, concat_axis=0, tiled=True),
        lax.all_to_all(value_slots, "seq", split_axis=1, concat_axis=0, tiled=True),
    )
    own_limit = lax.dynamic_slice_in_dim(slot_limit, device_index * per_device, per_device)
    key_place = jnp.arange(length, dtype=jnp.int32)
    key_bias = jnp.where(key_place[:, None] < own_limit[None, :], 0.0, neg_large).astype(
        jnp.float32
    )
    combined = attend_all(
        query_all.reshape(length, per_device, HDIM),
        key_all.reshape(length, per_device, HDIM),
        value_all.reshape(length, per_device, HDIM),
        key_bias,
    )
    combined = combined.reshape(length, 1, per_device, HDIM)
    returned = lax.all_to_all(combined, "seq", split_axis=0, concat_axis=1, tiled=True)
    return returned.reshape(tokens, seq_count, feature_dim)


def partner_of(me, step, count):
    place, other = 1, 0
    while place < count:
        other = other + ((me // place + (step // place) % 2) % 2) * place
        place *= 2
    return other


def fused(count, own_heads, clip_ref, q_ref, k_ref, v_ref, o_ref,
          held, wide, result, frames_ref, frames_sem, send_sem, recv_sem, osend_sem, orecv_sem, round_sem):
    tokens, clips, _ = q_ref.shape
    length = tokens * count
    me = lax.axis_index("seq")
    half = count // 2
    bits = [1 << bit for bit in range(half.bit_length())]
    order = sorted(range(1, count), key=lambda step: (step < half, step < half or step // 2 % 2 == 0))
    others = [partner_of(me, step, count) for step in order]
    sources = (k_ref, q_ref, v_ref)

    barrier = pltpu.get_barrier_semaphore()
    for bit in bits:
        pl.semaphore_signal(barrier, inc=1, device_id={"seq": partner_of(me, bit, count)})

    def columns(owner, head):
        return pl.ds(pl.multiple_of((owner * own_heads + head) * HDIM, HDIM), HDIM)

    own_rows = pl.ds(me * tokens, tokens)

    def send(head, steps):
        for step in steps:
            other = partner_of(me, step, count)
            for which, source in enumerate(sources):
                pltpu.make_async_remote_copy(
                    src_ref=source.at[:, :, columns(other, head)],
                    dst_ref=held.at[head, which, own_rows],
                    send_sem=send_sem.at[head, which],
                    recv_sem=recv_sem.at[head, which],
                    device_id={"seq": other},
                ).start()

    pl.semaphore_wait(barrier, len(bits))
    known = [0]
    ready = [half]
    for turn, bit in enumerate(reversed(bits[:-1])):
        pl.semaphore_signal(
            round_sem.at[turn], inc=1, device_id={"seq": partner_of(me, bit, count)}
        )
        send(0, ready)
        if turn == 0:
            for head in range(1, own_heads):
                send(head, ready)
        pl.semaphore_wait(round_sem.at[turn], 1)
        fresh = [low + bit for low in known]
        ready = [half + low for low in fresh]
        known = known + fresh
    send(0, ready)
    send(0, range(1, half))
    for head in range(1, own_heads):
        send(head, [step for step in order if step != half])

    frames_copy = pltpu.make_async_copy(clip_ref, frames_ref, frames_sem.at[0])
    frames_copy.start()
    for head in range(own_heads):
        for which, source in enumerate(sources):
            pltpu.make_async_copy(
                source.at[:, :, columns(me, head)],
                held.at[head, which, own_rows],
                recv_sem.at[head, which],
            ).start()
    place = lax.broadcasted_iota(jnp.int32, (length, length), 1)

    frames_copy.wait()

    def arrived(head, which):
        whole = held.at[head, which]
        pltpu.make_async_copy(whole, whole, recv_sem.at[head, which]).wait()
        wide[which] = whole[...].astype(jnp.float32).reshape(length * clips, HDIM)

    def rows(which, clip):
        return wide[which, pl.ds(clip, length, stride=clips), :].astype(jnp.bfloat16)

    for head in range(own_heads):
        arrived(head, 0)
        arrived(head, 1)
        weights = []
        for clip in range(clips):
            scores = lax.dot_general(
                rows(1, clip), rows(0, clip), (((1,), (1,)), ((), ())),
                preferred_element_type=jnp.float32,
            ) * (1.0 / math.sqrt(HDIM))
            scores = jnp.where(place < frames_ref[clip] * (length // FRAMES), scores, -jnp.inf)
            exponent = jnp.exp(scores - jnp.max(scores, axis=1, keepdims=True))
            weights.append(
                (exponent / jnp.sum(exponent, axis=1, keepdims=True)).astype(jnp.bfloat16)
            )
        arrived(head, 2)
        for clip in range(clips):
            wide[3, pl.ds(clip, length, stride=clips), :] = jnp.dot(
                weights[clip], rows(2, clip), preferred_element_type=jnp.float32
            )
        result[head] = wide[3].reshape(length, clips, HDIM).astype(jnp.bfloat16)
        for other in others:
            pltpu.make_async_remote_copy(
                src_ref=result.at[head, pl.ds(other * tokens, tokens)],
                dst_ref=o_ref.at[:, :, columns(me, head)],
                send_sem=osend_sem.at[head],
                recv_sem=orecv_sem.at[0],
                device_id={"seq": other},
            ).start()
        pltpu.make_async_copy(
            result.at[head, own_rows], o_ref.at[:, :, columns(me, head)], orecv_sem.at[0]
        ).start()

    sent = held.at[0, 0, pl.ds(0, length - tokens)]
    for head in range(own_heads):
        for which in range(3):
            pltpu.make_async_copy(sent, sent, send_sem.at[head, which]).wait()
        pltpu.make_async_copy(sent, sent, osend_sem.at[head]).wait()
    pltpu.make_async_copy(o_ref, o_ref, orecv_sem.at[0]).wait()


def fused_body(queries, keys, values, clip_frames):
    tokens, clips, features = queries.shape
    count = lax.axis_size("seq")
    own_heads = HEADS // count
    length = tokens * count
    return pl.pallas_call(
        functools.partial(fused, count, own_heads),
        out_shape=pltpu.VMEM(queries.shape, jnp.bfloat16),
        in_specs=[pl.BlockSpec(memory_space=pl.ANY)] * 4,
        out_specs=pl.BlockSpec(memory_space=pltpu.VMEM),
        scratch_shapes=[
            pltpu.VMEM((own_heads, 3, length, clips, HDIM), jnp.bfloat16),
            pltpu.VMEM((4, length * clips, HDIM), jnp.float32),
            pltpu.VMEM((own_heads, length, clips, HDIM), jnp.bfloat16),
            pltpu.SMEM(clip_frames.shape, jnp.int32),
            pltpu.SemaphoreType.DMA((1,)),
            pltpu.SemaphoreType.DMA((own_heads, 3)),
            pltpu.SemaphoreType.DMA((own_heads, 3)),
            pltpu.SemaphoreType.DMA((own_heads,)),
            pltpu.SemaphoreType.DMA((1,)),
            pltpu.SemaphoreType.REGULAR((max(count.bit_length() - 2, 1),)),
        ],
        compiler_params=pltpu.CompilerParams(collective_id=0, has_side_effects=True),
    )(clip_frames, queries, keys, values)


def solution(mesh):
    split_heads = mesh.shape["seq"] > 2 and HEADS % mesh.shape["seq"] == 0
    return jax.shard_map(
        fused_body if split_heads else body,
        mesh=mesh,
        in_specs=(P("seq", "grp", None), P("seq", "grp", None), P("seq", "grp", None), P("grp")),
        out_specs=P("seq", "grp", None),
        check_vma=False,
    )
```

```python
import functools
import math

import jax
import jax.numpy as jnp
from jax import lax
from jax.experimental import pallas as pl
from jax.experimental.pallas import tpu as pltpu
from jax.sharding import PartitionSpec as P

HEADS = 32
HDIM = 128
FRAMES = 8

OPENING = ('b', 'c', 'c', 'b')
ORDERS = {
    'first': ('anc', 'abn', 'anb', 'cna'),
    'later': ('bnac', 'bcna', 'cban', 'cban'),
    'return': ('bcan', 'bcan', 'bcan', 'bcan'),
    'last': ('canb', 'bcan', 'bcan', 'canb'),
}


neg_large = -1e30


def attend_block(query_block, key_rows, value_rows, key_bias):
    scores = jnp.einsum("qnd,knd->nqk", query_block, key_rows, preferred_element_type=jnp.float32)
    scores = scores * (1.0 / math.sqrt(HDIM)) + jnp.transpose(key_bias)[:, None, :]
    row_max = jnp.max(scores, axis=2, keepdims=True)
    exponent = jnp.exp(scores - row_max)
    weights = (exponent / jnp.sum(exponent, axis=2, keepdims=True)).astype(jnp.bfloat16)
    combined = jnp.einsum("nqk,knd->qnd", weights, value_rows, preferred_element_type=jnp.float32)
    return combined.astype(jnp.bfloat16)


def attend_all(query_rows, key_rows, value_rows, key_bias):
    length, item_count, head_dim = query_rows.shape
    block_rows = min(512, length)
    blocked = query_rows.reshape(length // block_rows, block_rows, item_count, head_dim)
    combined = lax.map(
        lambda query_block: attend_block(query_block, key_rows, value_rows, key_bias), blocked
    )
    return combined.reshape(length, item_count, head_dim)


def body(queries, keys, values, clip_frames):
    tokens, seq_count, feature_dim = queries.shape
    devices = lax.axis_size("seq")
    device_index = lax.axis_index("seq")
    slot_count = seq_count * HEADS
    per_device = slot_count // devices
    length = tokens * devices
    frame_tokens = length // FRAMES
    query_slots = queries.reshape(tokens, devices, per_device, HDIM)
    key_slots = keys.reshape(tokens, devices, per_device, HDIM)
    value_slots = values.reshape(tokens, devices, per_device, HDIM)
    slot_limit = jnp.repeat(clip_frames * frame_tokens, HEADS)
    query_all, key_all, value_all = (
        lax.all_to_all(query_slots, "seq", split_axis=1, concat_axis=0, tiled=True),
        lax.all_to_all(key_slots, "seq", split_axis=1, concat_axis=0, tiled=True),
        lax.all_to_all(value_slots, "seq", split_axis=1, concat_axis=0, tiled=True),
    )
    own_limit = lax.dynamic_slice_in_dim(slot_limit, device_index * per_device, per_device)
    key_place = jnp.arange(length, dtype=jnp.int32)
    key_bias = jnp.where(key_place[:, None] < own_limit[None, :], 0.0, neg_large).astype(
        jnp.float32
    )
    combined = attend_all(
        query_all.reshape(length, per_device, HDIM),
        key_all.reshape(length, per_device, HDIM),
        value_all.reshape(length, per_device, HDIM),
        key_bias,
    )
    combined = combined.reshape(length, 1, per_device, HDIM)
    returned = lax.all_to_all(combined, "seq", split_axis=0, concat_axis=1, tiled=True)
    return returned.reshape(tokens, seq_count, feature_dim)


def fused(count, own_heads, clip_ref, q_ref, k_ref, v_ref, o_ref,
          held, wide, result, frames_ref, frames_sem, send_sem, recv_sem, osend_sem, orecv_sem, round_sem, reply_sem):
    tokens, clips, _ = q_ref.shape
    length = tokens * count
    me = lax.axis_index("seq")
    quarter = count // 4
    layer = me // quarter
    last = layer // 3
    flips = [(1 - 2 * (me // (1 << bit) % 2)) * (1 << bit) for bit in range(count.bit_length() - 1)]
    mates = range(quarter.bit_length() - 1)
    lows = sorted(range(quarter), key=lambda low: low // 2 % 2 == 0)
    sources = (k_ref, q_ref, v_ref)

    def flipped(mask):
        return sum(flip for bit, flip in enumerate(flips) if mask >> bit & 1)

    leads = {"n": 0, "a": quarter, "b": 2 * quarter, "c": 3 * quarter}

    def pick(masks):
        value = flipped(masks[3])
        for index in range(3):
            if masks[index] != masks[3]:
                value = jnp.where(layer == index, flipped(masks[index]), value)
        return me + value

    def sequence(words):
        plans = [[leads[block] + low for block in word for low in lows] for word in words]
        return [pick(masks) for masks in zip(*[[mask for mask in plan if mask] for plan in plans])]

    barrier = pltpu.get_barrier_semaphore()
    for bit in mates:
        pl.semaphore_signal(barrier, inc=1, device_id={"seq": me + flips[bit]})

    @pl.when(last == 0)
    def _():
        for block in "abc":
            pl.semaphore_signal(barrier, inc=1, device_id={"seq": me + flipped(leads[block])})

    opening = [pick([leads[block] + low for block in OPENING]) for low in range(quarter)]

    def columns(owner, head):
        return pl.ds(pl.multiple_of((owner * own_heads + head) * HDIM, HDIM), HDIM)

    own_rows = pl.ds(me * tokens, tokens)

    def send(head, others):
        for which, source in enumerate(sources):
            for other in others:
                pltpu.make_async_remote_copy(
                    src_ref=source.at[:, :, columns(other, head)],
                    dst_ref=held.at[head, which, own_rows],
                    send_sem=send_sem.at[head, which],
                    recv_sem=recv_sem.at[head, which],
                    device_id={"seq": other},
                ).start()

    pl.semaphore_wait(barrier, len(mates) + 2 + last)

    @pl.when(last == 1)
    def _():
        for block in "abc":
            pl.semaphore_signal(reply_sem.at[0], inc=1, device_id={"seq": me + flipped(leads[block])})

    send(0, opening[:1])
    for bit in mates:
        pl.semaphore_signal(round_sem.at[0, bit], inc=1, device_id={"seq": me + flips[bit]})
        pl.semaphore_wait(round_sem.at[0, bit], 1)
        send(0, opening[1 << bit : 2 << bit])

    @pl.when(last == 0)
    def _():
        pl.semaphore_wait(reply_sem.at[0], 1)

    for bit in mates:
        pl.semaphore_signal(round_sem.at[1, bit], inc=1, device_id={"seq": me + flips[bit]})
        pl.semaphore_wait(round_sem.at[1, bit], 1)
    send(0, sequence(ORDERS["first"]))
    for head in range(1, own_heads):
        send(head, sequence(ORDERS["later"]))

    frames_copy = pltpu.make_async_copy(clip_ref, frames_ref, frames_sem.at[0])
    frames_copy.start()
    for head in range(own_heads):
        for which, source in enumerate(sources):
            pltpu.make_async_copy(
                source.at[:, :, columns(me, head)],
                held.at[head, which, own_rows],
                recv_sem.at[head, which],
            ).start()
    place = lax.broadcasted_iota(jnp.int32, (length, length), 1)

    frames_copy.wait()

    def arrived(head, which):
        whole = held.at[head, which]
        pltpu.make_async_copy(whole, whole, recv_sem.at[head, which]).wait()
        wide[which] = whole[...].astype(jnp.float32).reshape(length * clips, HDIM)

    def rows(which, clip):
        return wide[which, pl.ds(clip, length, stride=clips), :].astype(jnp.bfloat16)

    for head in range(own_heads):
        arrived(head, 0)
        arrived(head, 1)
        weights = []
        for clip in range(clips):
            scores = lax.dot_general(
                rows(1, clip), rows(0, clip), (((1,), (1,)), ((), ())),
                preferred_element_type=jnp.float32,
            ) * (1.0 / math.sqrt(HDIM))
            scores = jnp.where(place < frames_ref[clip] * (length // FRAMES), scores, -jnp.inf)
            exponent = jnp.exp(scores - jnp.max(scores, axis=1, keepdims=True))
            weights.append(
                (exponent / jnp.sum(exponent, axis=1, keepdims=True)).astype(jnp.bfloat16)
            )
        arrived(head, 2)
        for clip in range(clips):
            wide[3, pl.ds(clip, length, stride=clips), :] = jnp.dot(
                weights[clip], rows(2, clip), preferred_element_type=jnp.float32
            )
        result[head] = wide[3].reshape(length, clips, HDIM).astype(jnp.bfloat16)
        for other in sequence(ORDERS["return" if head + 1 < own_heads else "last"]):
            pltpu.make_async_remote_copy(
                src_ref=result.at[head, pl.ds(other * tokens, tokens)],
                dst_ref=o_ref.at[:, :, columns(me, head)],
                send_sem=osend_sem.at[head],
                recv_sem=orecv_sem.at[0],
                device_id={"seq": other},
            ).start()
        pltpu.make_async_copy(
            result.at[head, own_rows], o_ref.at[:, :, columns(me, head)], orecv_sem.at[0]
        ).start()

    sent = held.at[0, 0, pl.ds(0, length - tokens)]
    for head in range(own_heads):
        for which in range(3):
            pltpu.make_async_copy(sent, sent, send_sem.at[head, which]).wait()
        pltpu.make_async_copy(sent, sent, osend_sem.at[head]).wait()
    pltpu.make_async_copy(o_ref, o_ref, orecv_sem.at[0]).wait()


def fused_body(queries, keys, values, clip_frames):
    tokens, clips, features = queries.shape
    count = lax.axis_size("seq")
    own_heads = HEADS // count
    length = tokens * count
    return pl.pallas_call(
        functools.partial(fused, count, own_heads),
        out_shape=pltpu.VMEM(queries.shape, jnp.bfloat16),
        in_specs=[pl.BlockSpec(memory_space=pl.ANY)] * 4,
        out_specs=pl.BlockSpec(memory_space=pltpu.VMEM),
        scratch_shapes=[
            pltpu.VMEM((own_heads, 3, length, clips, HDIM), jnp.bfloat16),
            pltpu.VMEM((4, length * clips, HDIM), jnp.float32),
            pltpu.VMEM((own_heads, length, clips, HDIM), jnp.bfloat16),
            pltpu.SMEM(clip_frames.shape, jnp.int32),
            pltpu.SemaphoreType.DMA((1,)),
            pltpu.SemaphoreType.DMA((own_heads, 3)),
            pltpu.SemaphoreType.DMA((own_heads, 3)),
            pltpu.SemaphoreType.DMA((own_heads,)),
            pltpu.SemaphoreType.DMA((1,)),
            pltpu.SemaphoreType.REGULAR((2, count.bit_length())),
            pltpu.SemaphoreType.REGULAR((1,)),
        ],
        compiler_params=pltpu.CompilerParams(collective_id=0, has_side_effects=True),
    )(clip_frames, queries, keys, values)


def solution(mesh):
    split_heads = mesh.shape["seq"] >= 8 and HEADS % mesh.shape["seq"] == 0
    return jax.shard_map(
        fused_body if split_heads else body,
        mesh=mesh,
        in_specs=(P("seq", "grp", None), P("seq", "grp", None), P("seq", "grp", None), P("grp")),
        out_specs=P("seq", "grp", None),
        check_vma=False,
    )
```

```python
import functools
import math

import jax
import jax.numpy as jnp
from jax import lax
from jax.experimental import pallas as pl
from jax.experimental.pallas import tpu as pltpu
from jax.sharding import PartitionSpec as P

HEADS = 32
HDIM = 128
FRAMES = 8

OPENING = ('b', 'c', 'c', 'b')
ORDERS = {
    'first': ('anc', 'abn', 'anb', 'cna'),
    'later': ('bnac', 'bcna', 'cban', 'cban'),
    'return': ('bcan', 'bcan', 'bcan', 'bcan'),
    'last': ('canb', 'bcan', 'bcan', 'canb'),
}


neg_large = -1e30


def attend_block(query_block, key_rows, value_rows, key_bias):
    scores = jnp.einsum("qnd,knd->nqk", query_block, key_rows, preferred_element_type=jnp.float32)
    scores = scores * (1.0 / math.sqrt(HDIM)) + jnp.transpose(key_bias)[:, None, :]
    row_max = jnp.max(scores, axis=2, keepdims=True)
    exponent = jnp.exp(scores - row_max)
    weights = (exponent / jnp.sum(exponent, axis=2, keepdims=True)).astype(jnp.bfloat16)
    combined = jnp.einsum("nqk,knd->qnd", weights, value_rows, preferred_element_type=jnp.float32)
    return combined.astype(jnp.bfloat16)


def attend_all(query_rows, key_rows, value_rows, key_bias):
    length, item_count, head_dim = query_rows.shape
    block_rows = min(512, length)
    blocked = query_rows.reshape(length // block_rows, block_rows, item_count, head_dim)
    combined = lax.map(
        lambda query_block: attend_block(query_block, key_rows, value_rows, key_bias), blocked
    )
    return combined.reshape(length, item_count, head_dim)


def body(queries, keys, values, clip_frames):
    tokens, seq_count, feature_dim = queries.shape
    devices = lax.axis_size("seq")
    device_index = lax.axis_index("seq")
    slot_count = seq_count * HEADS
    per_device = slot_count // devices
    length = tokens * devices
    frame_tokens = length // FRAMES
    query_slots = queries.reshape(tokens, devices, per_device, HDIM)
    key_slots = keys.reshape(tokens, devices, per_device, HDIM)
    value_slots = values.reshape(tokens, devices, per_device, HDIM)
    slot_limit = jnp.repeat(clip_frames * frame_tokens, HEADS)
    query_all, key_all, value_all = (
        lax.all_to_all(query_slots, "seq", split_axis=1, concat_axis=0, tiled=True),
        lax.all_to_all(key_slots, "seq", split_axis=1, concat_axis=0, tiled=True),
        lax.all_to_all(value_slots, "seq", split_axis=1, concat_axis=0, tiled=True),
    )
    own_limit = lax.dynamic_slice_in_dim(slot_limit, device_index * per_device, per_device)
    key_place = jnp.arange(length, dtype=jnp.int32)
    key_bias = jnp.where(key_place[:, None] < own_limit[None, :], 0.0, neg_large).astype(
        jnp.float32
    )
    combined = attend_all(
        query_all.reshape(length, per_device, HDIM),
        key_all.reshape(length, per_device, HDIM),
        value_all.reshape(length, per_device, HDIM),
        key_bias,
    )
    combined = combined.reshape(length, 1, per_device, HDIM)
    returned = lax.all_to_all(combined, "seq", split_axis=0, concat_axis=1, tiled=True)
    return returned.reshape(tokens, seq_count, feature_dim)


def fused(count, own_heads, clip_ref, q_ref, k_ref, v_ref, o_ref,
          held, wide, result, staged, staged_sem, frames_ref, frames_sem, send_sem, recv_sem, osend_sem, orecv_sem, round_sem, reply_sem):
    tokens, clips, _ = q_ref.shape
    length = tokens * count
    me = lax.axis_index("seq")
    quarter = count // 4
    layer = me // quarter
    last = layer // 3
    flips = [(1 - 2 * (me // (1 << bit) % 2)) * (1 << bit) for bit in range(count.bit_length() - 1)]
    mates = range(quarter.bit_length() - 1)
    lows = sorted(range(quarter), key=lambda low: low // 2 % 2 == 0)
    sources = (k_ref, q_ref, v_ref)

    def flipped(mask):
        return sum(flip for bit, flip in enumerate(flips) if mask >> bit & 1)

    leads = {"n": 0, "a": quarter, "b": 2 * quarter, "c": 3 * quarter}

    def pick(masks):
        value = flipped(masks[3])
        for index in range(3):
            if masks[index] != masks[3]:
                value = jnp.where(layer == index, flipped(masks[index]), value)
        return me + value

    def sequence(words):
        plans = [[leads[block] + low for block in word for low in lows] for word in words]
        return [pick(masks) for masks in zip(*[[mask for mask in plan if mask] for plan in plans])]

    loads = [
        pltpu.make_async_copy(source, staged.at[which], staged_sem.at[which])
        for which, source in enumerate(sources)
    ]
    for load in loads:
        load.start()
    barrier = pltpu.get_barrier_semaphore()
    for bit in mates:
        pl.semaphore_signal(barrier, inc=1, device_id={"seq": me + flips[bit]})

    @pl.when(last == 0)
    def _():
        for block in "abc":
            pl.semaphore_signal(barrier, inc=1, device_id={"seq": me + flipped(leads[block])})

    opening = [pick([leads[block] + low for block in OPENING]) for low in range(quarter)]

    def columns(owner, head):
        return pl.ds(pl.multiple_of((owner * own_heads + head) * HDIM, HDIM), HDIM)

    own_rows = pl.ds(me * tokens, tokens)

    def send(head, others):
        for which in range(3):
            for other in others:
                pltpu.make_async_remote_copy(
                    src_ref=staged.at[which, :, :, columns(other, head)],
                    dst_ref=held.at[head, which, own_rows],
                    send_sem=send_sem.at[head, which],
                    recv_sem=recv_sem.at[head, which],
                    device_id={"seq": other},
                ).start()

    pl.semaphore_wait(barrier, len(mates) + 2 + last)

    @pl.when(last == 1)
    def _():
        for block in "abc":
            pl.semaphore_signal(reply_sem.at[0], inc=1, device_id={"seq": me + flipped(leads[block])})

    for load in loads:
        load.wait()
    send(0, opening[:1])
    for bit in mates:
        pl.semaphore_signal(round_sem.at[0, bit], inc=1, device_id={"seq": me + flips[bit]})
        pl.semaphore_wait(round_sem.at[0, bit], 1)
        send(0, opening[1 << bit : 2 << bit])

    @pl.when(last == 0)
    def _():
        pl.semaphore_wait(reply_sem.at[0], 1)

    for bit in mates:
        pl.semaphore_signal(round_sem.at[1, bit], inc=1, device_id={"seq": me + flips[bit]})
        pl.semaphore_wait(round_sem.at[1, bit], 1)
    send(0, sequence(ORDERS["first"]))
    for head in range(1, own_heads):
        send(head, sequence(ORDERS["later"]))

    frames_copy = pltpu.make_async_copy(clip_ref, frames_ref, frames_sem.at[0])
    frames_copy.start()
    for head in range(own_heads):
        for which, source in enumerate(sources):
            pltpu.make_async_copy(
                source.at[:, :, columns(me, head)],
                held.at[head, which, own_rows],
                recv_sem.at[head, which],
            ).start()
    place = lax.broadcasted_iota(jnp.int32, (length, length), 1)

    frames_copy.wait()

    def arrived(head, which):
        whole = held.at[head, which]
        pltpu.make_async_copy(whole, whole, recv_sem.at[head, which]).wait()
        wide[which] = whole[...].astype(jnp.float32).reshape(length * clips, HDIM)

    def rows(which, clip):
        return wide[which, pl.ds(clip, length, stride=clips), :].astype(jnp.bfloat16)

    for head in range(own_heads):
        arrived(head, 0)
        arrived(head, 1)
        weights = []
        for clip in range(clips):
            scores = lax.dot_general(
                rows(1, clip), rows(0, clip), (((1,), (1,)), ((), ())),
                preferred_element_type=jnp.float32,
            ) * (1.0 / math.sqrt(HDIM))
            scores = jnp.where(place < frames_ref[clip] * (length // FRAMES), scores, -jnp.inf)
            exponent = jnp.exp(scores - jnp.max(scores, axis=1, keepdims=True))
            weights.append(
                (exponent / jnp.sum(exponent, axis=1, keepdims=True)).astype(jnp.bfloat16)
            )
        arrived(head, 2)
        for clip in range(clips):
            wide[3, pl.ds(clip, length, stride=clips), :] = jnp.dot(
                weights[clip], rows(2, clip), preferred_element_type=jnp.float32
            )
        result[head] = wide[3].reshape(length, clips, HDIM).astype(jnp.bfloat16)
        for other in sequence(ORDERS["return" if head + 1 < own_heads else "last"]):
            pltpu.make_async_remote_copy(
                src_ref=result.at[head, pl.ds(other * tokens, tokens)],
                dst_ref=o_ref.at[:, :, columns(me, head)],
                send_sem=osend_sem.at[head],
                recv_sem=orecv_sem.at[0],
                device_id={"seq": other},
            ).start()
        pltpu.make_async_copy(
            result.at[head, own_rows], o_ref.at[:, :, columns(me, head)], orecv_sem.at[0]
        ).start()

    sent = held.at[0, 0, pl.ds(0, length - tokens)]
    for head in range(own_heads):
        for which in range(3):
            pltpu.make_async_copy(sent, sent, send_sem.at[head, which]).wait()
        pltpu.make_async_copy(sent, sent, osend_sem.at[head]).wait()
    pltpu.make_async_copy(o_ref, o_ref, orecv_sem.at[0]).wait()


def fused_body(queries, keys, values, clip_frames):
    tokens, clips, features = queries.shape
    count = lax.axis_size("seq")
    own_heads = HEADS // count
    length = tokens * count
    return pl.pallas_call(
        functools.partial(fused, count, own_heads),
        out_shape=pltpu.VMEM(queries.shape, jnp.bfloat16),
        in_specs=[pl.BlockSpec(memory_space=pl.ANY)] * 4,
        out_specs=pl.BlockSpec(memory_space=pltpu.VMEM),
        scratch_shapes=[
            pltpu.VMEM((own_heads, 3, length, clips, HDIM), jnp.bfloat16),
            pltpu.VMEM((4, length * clips, HDIM), jnp.float32),
            pltpu.VMEM((own_heads, length, clips, HDIM), jnp.bfloat16),
            pltpu.VMEM((3,) + queries.shape, jnp.bfloat16),
            pltpu.SemaphoreType.DMA((3,)),
            pltpu.SMEM(clip_frames.shape, jnp.int32),
            pltpu.SemaphoreType.DMA((1,)),
            pltpu.SemaphoreType.DMA((own_heads, 3)),
            pltpu.SemaphoreType.DMA((own_heads, 3)),
            pltpu.SemaphoreType.DMA((own_heads,)),
            pltpu.SemaphoreType.DMA((1,)),
            pltpu.SemaphoreType.REGULAR((2, count.bit_length())),
            pltpu.SemaphoreType.REGULAR((1,)),
        ],
        compiler_params=pltpu.CompilerParams(collective_id=0, has_side_effects=True),
    )(clip_frames, queries, keys, values)


def solution(mesh):
    split_heads = mesh.shape["seq"] >= 8 and HEADS % mesh.shape["seq"] == 0
    return jax.shard_map(
        fused_body if split_heads else body,
        mesh=mesh,
        in_specs=(P("seq", "grp", None), P("seq", "grp", None), P("seq", "grp", None), P("grp")),
        out_specs=P("seq", "grp", None),
        check_vma=False,
    )
```

```python
import functools
import math

import jax
import jax.numpy as jnp
from jax import lax
from jax.experimental import pallas as pl
from jax.experimental.pallas import tpu as pltpu
from jax.sharding import PartitionSpec as P

HEADS = 32
HDIM = 128
FRAMES = 8

OPENING = ('b', 'c', 'c', 'b')
ORDERS = {
    'first': ('anc', 'abn', 'anb', 'cna'),
    'later': ('bnac', 'bcna', 'cban', 'cban'),
    'return': ('bcan', 'bcan', 'bcan', 'bcan'),
    'last': ('canb', 'bcan', 'bcan', 'canb'),
}


neg_large = -1e30


def attend_block(query_block, key_rows, value_rows, key_bias):
    scores = jnp.einsum("qnd,knd->nqk", query_block, key_rows, preferred_element_type=jnp.float32)
    scores = scores * (1.0 / math.sqrt(HDIM)) + jnp.transpose(key_bias)[:, None, :]
    row_max = jnp.max(scores, axis=2, keepdims=True)
    exponent = jnp.exp(scores - row_max)
    weights = (exponent / jnp.sum(exponent, axis=2, keepdims=True)).astype(jnp.bfloat16)
    combined = jnp.einsum("nqk,knd->qnd", weights, value_rows, preferred_element_type=jnp.float32)
    return combined.astype(jnp.bfloat16)


def attend_all(query_rows, key_rows, value_rows, key_bias):
    length, item_count, head_dim = query_rows.shape
    block_rows = min(512, length)
    blocked = query_rows.reshape(length // block_rows, block_rows, item_count, head_dim)
    combined = lax.map(
        lambda query_block: attend_block(query_block, key_rows, value_rows, key_bias), blocked
    )
    return combined.reshape(length, item_count, head_dim)


def body(queries, keys, values, clip_frames):
    tokens, seq_count, feature_dim = queries.shape
    devices = lax.axis_size("seq")
    device_index = lax.axis_index("seq")
    slot_count = seq_count * HEADS
    per_device = slot_count // devices
    length = tokens * devices
    frame_tokens = length // FRAMES
    query_slots = queries.reshape(tokens, devices, per_device, HDIM)
    key_slots = keys.reshape(tokens, devices, per_device, HDIM)
    value_slots = values.reshape(tokens, devices, per_device, HDIM)
    slot_limit = jnp.repeat(clip_frames * frame_tokens, HEADS)
    query_all, key_all, value_all = (
        lax.all_to_all(query_slots, "seq", split_axis=1, concat_axis=0, tiled=True),
        lax.all_to_all(key_slots, "seq", split_axis=1, concat_axis=0, tiled=True),
        lax.all_to_all(value_slots, "seq", split_axis=1, concat_axis=0, tiled=True),
    )
    own_limit = lax.dynamic_slice_in_dim(slot_limit, device_index * per_device, per_device)
    key_place = jnp.arange(length, dtype=jnp.int32)
    key_bias = jnp.where(key_place[:, None] < own_limit[None, :], 0.0, neg_large).astype(
        jnp.float32
    )
    combined = attend_all(
        query_all.reshape(length, per_device, HDIM),
        key_all.reshape(length, per_device, HDIM),
        value_all.reshape(length, per_device, HDIM),
        key_bias,
    )
    combined = combined.reshape(length, 1, per_device, HDIM)
    returned = lax.all_to_all(combined, "seq", split_axis=0, concat_axis=1, tiled=True)
    return returned.reshape(tokens, seq_count, feature_dim)


def fused(count, own_heads, clip_ref, q_ref, k_ref, v_ref, o_ref,
          held, wide, result, staged, staged_sem, frames_ref, frames_sem, send_sem, recv_sem, osend_sem, orecv_sem, round_sem, reply_sem):
    tokens, clips, _ = q_ref.shape
    length = tokens * count
    me = lax.axis_index("seq")
    quarter = count // 4
    layer = me // quarter
    last = layer // 3
    flips = [(1 - 2 * (me // (1 << bit) % 2)) * (1 << bit) for bit in range(count.bit_length() - 1)]
    mates = range(quarter.bit_length() - 1)
    lows = sorted(range(quarter), key=lambda low: low // 2 % 2 == 0)
    sources = (k_ref, q_ref, v_ref)

    def flipped(mask):
        return sum(flip for bit, flip in enumerate(flips) if mask >> bit & 1)

    leads = {"n": 0, "a": quarter, "b": 2 * quarter, "c": 3 * quarter}

    def pick(masks):
        value = flipped(masks[3])
        for index in range(3):
            if masks[index] != masks[3]:
                value = jnp.where(layer == index, flipped(masks[index]), value)
        return me + value

    def sequence(words):
        plans = [[leads[block] + low for block in word for low in lows] for word in words]
        return [pick(masks) for masks in zip(*[[mask for mask in plan if mask] for plan in plans])]

    loads = [
        pltpu.make_async_copy(source, staged.at[which], staged_sem.at[which])
        for which, source in enumerate(sources)
    ]
    for load in loads:
        load.start()
    barrier = pltpu.get_barrier_semaphore()
    for bit in mates:
        pl.semaphore_signal(barrier, inc=1, device_id={"seq": me + flips[bit]})

    @pl.when(last == 0)
    def _():
        for block in "abc":
            pl.semaphore_signal(barrier, inc=1, device_id={"seq": me + flipped(leads[block])})

    opening = [pick([leads[block] + low for block in OPENING]) for low in range(quarter)]

    def columns(owner, head):
        return pl.ds(pl.multiple_of((owner * own_heads + head) * HDIM, HDIM), HDIM)

    own_rows = pl.ds(me * tokens, tokens)

    def send(head, others, loads=()):
        for which in range(3):
            for load in loads[which : which + 1]:
                load.wait()
            for other in others:
                pltpu.make_async_remote_copy(
                    src_ref=staged.at[which, :, :, columns(other, head)],
                    dst_ref=held.at[head, which, own_rows],
                    send_sem=send_sem.at[head, which],
                    recv_sem=recv_sem.at[head, which],
                    device_id={"seq": other},
                ).start()

    pl.semaphore_wait(barrier, len(mates) + 2 + last)

    @pl.when(last == 1)
    def _():
        for block in "abc":
            pl.semaphore_signal(reply_sem.at[0], inc=1, device_id={"seq": me + flipped(leads[block])})

    send(0, opening[:1], loads)
    for bit in mates:
        pl.semaphore_signal(round_sem.at[0, bit], inc=1, device_id={"seq": me + flips[bit]})
        pl.semaphore_wait(round_sem.at[0, bit], 1)
        send(0, opening[1 << bit : 2 << bit])

    @pl.when(last == 0)
    def _():
        pl.semaphore_wait(reply_sem.at[0], 1)

    for bit in mates:
        pl.semaphore_signal(round_sem.at[1, bit], inc=1, device_id={"seq": me + flips[bit]})
        pl.semaphore_wait(round_sem.at[1, bit], 1)
    send(0, sequence(ORDERS["first"]))
    for head in range(1, own_heads):
        send(head, sequence(ORDERS["later"]))

    frames_copy = pltpu.make_async_copy(clip_ref, frames_ref, frames_sem.at[0])
    frames_copy.start()
    for head in range(own_heads):
        for which, source in enumerate(sources):
            pltpu.make_async_copy(
                source.at[:, :, columns(me, head)],
                held.at[head, which, own_rows],
                recv_sem.at[head, which],
            ).start()
    place = lax.broadcasted_iota(jnp.int32, (length, length), 1)

    frames_copy.wait()

    def arrived(head, which):
        whole = held.at[head, which]
        pltpu.make_async_copy(whole, whole, recv_sem.at[head, which]).wait()
        wide[which] = whole[...].astype(jnp.float32).reshape(length * clips, HDIM)

    def rows(which, clip):
        return wide[which, pl.ds(clip, length, stride=clips), :].astype(jnp.bfloat16)

    for head in range(own_heads):
        arrived(head, 0)
        arrived(head, 1)
        weights = []
        for clip in range(clips):
            scores = lax.dot_general(
                rows(1, clip), rows(0, clip), (((1,), (1,)), ((), ())),
                preferred_element_type=jnp.float32,
            ) * (1.0 / math.sqrt(HDIM))
            scores = jnp.where(place < frames_ref[clip] * (length // FRAMES), scores, -jnp.inf)
            exponent = jnp.exp(scores - jnp.max(scores, axis=1, keepdims=True))
            weights.append(
                (exponent / jnp.sum(exponent, axis=1, keepdims=True)).astype(jnp.bfloat16)
            )
        arrived(head, 2)
        for clip in range(clips):
            wide[3, pl.ds(clip, length, stride=clips), :] = jnp.dot(
                weights[clip], rows(2, clip), preferred_element_type=jnp.float32
            )
        result[head] = wide[3].reshape(length, clips, HDIM).astype(jnp.bfloat16)
        for other in sequence(ORDERS["return" if head + 1 < own_heads else "last"]):
            pltpu.make_async_remote_copy(
                src_ref=result.at[head, pl.ds(other * tokens, tokens)],
                dst_ref=o_ref.at[:, :, columns(me, head)],
                send_sem=osend_sem.at[head],
                recv_sem=orecv_sem.at[0],
                device_id={"seq": other},
            ).start()
        pltpu.make_async_copy(
            result.at[head, own_rows], o_ref.at[:, :, columns(me, head)], orecv_sem.at[0]
        ).start()

    sent = held.at[0, 0, pl.ds(0, length - tokens)]
    for head in range(own_heads):
        for which in range(3):
            pltpu.make_async_copy(sent, sent, send_sem.at[head, which]).wait()
        pltpu.make_async_copy(sent, sent, osend_sem.at[head]).wait()
    pltpu.make_async_copy(o_ref, o_ref, orecv_sem.at[0]).wait()


def fused_body(queries, keys, values, clip_frames):
    tokens, clips, features = queries.shape
    count = lax.axis_size("seq")
    own_heads = HEADS // count
    length = tokens * count
    return pl.pallas_call(
        functools.partial(fused, count, own_heads),
        out_shape=pltpu.VMEM(queries.shape, jnp.bfloat16),
        in_specs=[pl.BlockSpec(memory_space=pl.ANY)] * 4,
        out_specs=pl.BlockSpec(memory_space=pltpu.VMEM),
        scratch_shapes=[
            pltpu.VMEM((own_heads, 3, length, clips, HDIM), jnp.bfloat16),
            pltpu.VMEM((4, length * clips, HDIM), jnp.float32),
            pltpu.VMEM((own_heads, length, clips, HDIM), jnp.bfloat16),
            pltpu.VMEM((3,) + queries.shape, jnp.bfloat16),
            pltpu.SemaphoreType.DMA((3,)),
            pltpu.SMEM(clip_frames.shape, jnp.int32),
            pltpu.SemaphoreType.DMA((1,)),
            pltpu.SemaphoreType.DMA((own_heads, 3)),
            pltpu.SemaphoreType.DMA((own_heads, 3)),
            pltpu.SemaphoreType.DMA((own_heads,)),
            pltpu.SemaphoreType.DMA((1,)),
            pltpu.SemaphoreType.REGULAR((2, count.bit_length())),
            pltpu.SemaphoreType.REGULAR((1,)),
        ],
        compiler_params=pltpu.CompilerParams(collective_id=0, has_side_effects=True),
    )(clip_frames, queries, keys, values)


def solution(mesh):
    split_heads = mesh.shape["seq"] >= 8 and HEADS % mesh.shape["seq"] == 0
    return jax.shard_map(
        fused_body if split_heads else body,
        mesh=mesh,
        in_specs=(P("seq", "grp", None), P("seq", "grp", None), P("seq", "grp", None), P("grp")),
        out_specs=P("seq", "grp", None),
        check_vma=False,
    )
```

```python
import functools
import math

import jax
import jax.numpy as jnp
from jax import lax
from jax.experimental import pallas as pl
from jax.experimental.pallas import tpu as pltpu
from jax.sharding import PartitionSpec as P

HEADS = 32
HDIM = 128
FRAMES = 8

OPENING = ('b', 'c', 'c', 'b')
ORDERS = {
    'first': ('anc', 'abn', 'anb', 'cna'),
    'later': ('bnac', 'bcna', 'cban', 'cban'),
    'return': ('bcan', 'bcan', 'bcan', 'bcan'),
    'last': ('canb', 'bcan', 'bcan', 'canb'),
}


neg_large = -1e30


def attend_block(query_block, key_rows, value_rows, key_bias):
    scores = jnp.einsum("qnd,knd->nqk", query_block, key_rows, preferred_element_type=jnp.float32)
    scores = scores * (1.0 / math.sqrt(HDIM)) + jnp.transpose(key_bias)[:, None, :]
    row_max = jnp.max(scores, axis=2, keepdims=True)
    exponent = jnp.exp(scores - row_max)
    weights = (exponent / jnp.sum(exponent, axis=2, keepdims=True)).astype(jnp.bfloat16)
    combined = jnp.einsum("nqk,knd->qnd", weights, value_rows, preferred_element_type=jnp.float32)
    return combined.astype(jnp.bfloat16)


def attend_all(query_rows, key_rows, value_rows, key_bias):
    length, item_count, head_dim = query_rows.shape
    block_rows = min(512, length)
    blocked = query_rows.reshape(length // block_rows, block_rows, item_count, head_dim)
    combined = lax.map(
        lambda query_block: attend_block(query_block, key_rows, value_rows, key_bias), blocked
    )
    return combined.reshape(length, item_count, head_dim)


def body(queries, keys, values, clip_frames):
    tokens, seq_count, feature_dim = queries.shape
    devices = lax.axis_size("seq")
    device_index = lax.axis_index("seq")
    slot_count = seq_count * HEADS
    per_device = slot_count // devices
    length = tokens * devices
    frame_tokens = length // FRAMES
    query_slots = queries.reshape(tokens, devices, per_device, HDIM)
    key_slots = keys.reshape(tokens, devices, per_device, HDIM)
    value_slots = values.reshape(tokens, devices, per_device, HDIM)
    slot_limit = jnp.repeat(clip_frames * frame_tokens, HEADS)
    query_all, key_all, value_all = (
        lax.all_to_all(query_slots, "seq", split_axis=1, concat_axis=0, tiled=True),
        lax.all_to_all(key_slots, "seq", split_axis=1, concat_axis=0, tiled=True),
        lax.all_to_all(value_slots, "seq", split_axis=1, concat_axis=0, tiled=True),
    )
    own_limit = lax.dynamic_slice_in_dim(slot_limit, device_index * per_device, per_device)
    key_place = jnp.arange(length, dtype=jnp.int32)
    key_bias = jnp.where(key_place[:, None] < own_limit[None, :], 0.0, neg_large).astype(
        jnp.float32
    )
    combined = attend_all(
        query_all.reshape(length, per_device, HDIM),
        key_all.reshape(length, per_device, HDIM),
        value_all.reshape(length, per_device, HDIM),
        key_bias,
    )
    combined = combined.reshape(length, 1, per_device, HDIM)
    returned = lax.all_to_all(combined, "seq", split_axis=0, concat_axis=1, tiled=True)
    return returned.reshape(tokens, seq_count, feature_dim)


def fused(count, own_heads, clip_ref, q_ref, k_ref, v_ref, o_ref,
          held, wide, result, staged, staged_sem, frames_ref, frames_sem, send_sem, recv_sem, osend_sem, orecv_sem, round_sem, reply_sem):
    tokens, clips, _ = q_ref.shape
    length = tokens * count
    me = lax.axis_index("seq")
    quarter = count // 4
    layer = me // quarter
    last = layer // 3
    flips = [(1 - 2 * (me // (1 << bit) % 2)) * (1 << bit) for bit in range(count.bit_length() - 1)]
    mates = range(quarter.bit_length() - 1)
    lows = sorted(range(quarter), key=lambda low: low // 2 % 2 == 0)
    sources = (k_ref, q_ref, v_ref)

    def flipped(mask):
        return sum(flip for bit, flip in enumerate(flips) if mask >> bit & 1)

    leads = {"n": 0, "a": quarter, "b": 2 * quarter, "c": 3 * quarter}

    def pick(masks):
        value = flipped(masks[3])
        for index in range(3):
            if masks[index] != masks[3]:
                value = jnp.where(layer == index, flipped(masks[index]), value)
        return me + value

    def sequence(words):
        plans = [[leads[block] + low for block in word for low in lows] for word in words]
        return [pick(masks) for masks in zip(*[[mask for mask in plan if mask] for plan in plans])]

    loads = [
        pltpu.make_async_copy(source, staged.at[which], staged_sem.at[which])
        for which, source in enumerate(sources)
    ]
    for load in loads:
        load.start()
    barrier = pltpu.get_barrier_semaphore()
    for bit in mates:
        pl.semaphore_signal(barrier, inc=1, device_id={"seq": me + flips[bit]})

    @pl.when(last == 0)
    def _():
        for block in "abc":
            pl.semaphore_signal(barrier, inc=1, device_id={"seq": me + flipped(leads[block])})

    opening = [pick([leads[block] + low for block in OPENING]) for low in range(quarter)]

    def columns(owner, head):
        return pl.ds(pl.multiple_of((owner * own_heads + head) * HDIM, HDIM), HDIM)

    own_rows = pl.ds(me * tokens, tokens)

    def send(head, others, loads=()):
        for which in range(3):
            for load in loads[which : which + 1]:
                load.wait()
            for other in others:
                pltpu.make_async_remote_copy(
                    src_ref=staged.at[which, :, :, columns(other, head)],
                    dst_ref=held.at[head, which, own_rows],
                    send_sem=send_sem.at[head, which],
                    recv_sem=recv_sem.at[head, which],
                    device_id={"seq": other},
                ).start()

    pl.semaphore_wait(barrier, len(mates) + 2 + last)

    @pl.when(last == 1)
    def _():
        for block in "abc":
            pl.semaphore_signal(reply_sem.at[0], inc=1, device_id={"seq": me + flipped(leads[block])})

    send(0, opening[:1], loads)
    for bit in mates:
        pl.semaphore_signal(round_sem.at[0, bit], inc=1, device_id={"seq": me + flips[bit]})
        pl.semaphore_wait(round_sem.at[0, bit], 1)
        send(0, opening[1 << bit : 2 << bit])

    @pl.when(last == 0)
    def _():
        pl.semaphore_wait(reply_sem.at[0], 1)

    for bit in mates:
        pl.semaphore_signal(round_sem.at[1, bit], inc=1, device_id={"seq": me + flips[bit]})
        pl.semaphore_wait(round_sem.at[1, bit], 1)
    send(0, sequence(ORDERS["first"]))
    for head in range(1, own_heads):
        send(head, sequence(ORDERS["later"]))

    frames_copy = pltpu.make_async_copy(clip_ref, frames_ref, frames_sem.at[0])
    frames_copy.start()
    for head in range(own_heads):
        for which, source in enumerate(sources):
            pltpu.make_async_copy(
                staged.at[which, :, :, columns(me, head)],
                held.at[head, which, own_rows],
                recv_sem.at[head, which],
            ).start()
    place = lax.broadcasted_iota(jnp.int32, (length, length), 1)

    frames_copy.wait()

    def arrived(head, which):
        whole = held.at[head, which]
        pltpu.make_async_copy(whole, whole, recv_sem.at[head, which]).wait()
        wide[which] = whole[...].astype(jnp.float32).reshape(length * clips, HDIM)

    def rows(which, clip):
        return wide[which, pl.ds(clip, length, stride=clips), :].astype(jnp.bfloat16)

    for head in range(own_heads):
        arrived(head, 0)
        arrived(head, 1)
        weights = []
        for clip in range(clips):
            scores = lax.dot_general(
                rows(1, clip), rows(0, clip), (((1,), (1,)), ((), ())),
                preferred_element_type=jnp.float32,
            ) * (1.0 / math.sqrt(HDIM))
            scores = jnp.where(place < frames_ref[clip] * (length // FRAMES), scores, -jnp.inf)
            exponent = jnp.exp(scores - jnp.max(scores, axis=1, keepdims=True))
            weights.append(
                (exponent / jnp.sum(exponent, axis=1, keepdims=True)).astype(jnp.bfloat16)
            )
        arrived(head, 2)
        for clip in range(clips):
            wide[3, pl.ds(clip, length, stride=clips), :] = jnp.dot(
                weights[clip], rows(2, clip), preferred_element_type=jnp.float32
            )
        result[head] = wide[3].reshape(length, clips, HDIM).astype(jnp.bfloat16)
        for other in sequence(ORDERS["return" if head + 1 < own_heads else "last"]):
            pltpu.make_async_remote_copy(
                src_ref=result.at[head, pl.ds(other * tokens, tokens)],
                dst_ref=o_ref.at[:, :, columns(me, head)],
                send_sem=osend_sem.at[head],
                recv_sem=orecv_sem.at[0],
                device_id={"seq": other},
            ).start()
        pltpu.make_async_copy(
            result.at[head, own_rows], o_ref.at[:, :, columns(me, head)], orecv_sem.at[0]
        ).start()

    sent = held.at[0, 0, pl.ds(0, length - tokens)]
    for head in range(own_heads):
        for which in range(3):
            pltpu.make_async_copy(sent, sent, send_sem.at[head, which]).wait()
        pltpu.make_async_copy(sent, sent, osend_sem.at[head]).wait()
    pltpu.make_async_copy(o_ref, o_ref, orecv_sem.at[0]).wait()


def fused_body(queries, keys, values, clip_frames):
    tokens, clips, features = queries.shape
    count = lax.axis_size("seq")
    own_heads = HEADS // count
    length = tokens * count
    return pl.pallas_call(
        functools.partial(fused, count, own_heads),
        out_shape=pltpu.VMEM(queries.shape, jnp.bfloat16),
        in_specs=[pl.BlockSpec(memory_space=pl.ANY)] * 4,
        out_specs=pl.BlockSpec(memory_space=pltpu.VMEM),
        scratch_shapes=[
            pltpu.VMEM((own_heads, 3, length, clips, HDIM), jnp.bfloat16),
            pltpu.VMEM((4, length * clips, HDIM), jnp.float32),
            pltpu.VMEM((own_heads, length, clips, HDIM), jnp.bfloat16),
            pltpu.VMEM((3,) + queries.shape, jnp.bfloat16),
            pltpu.SemaphoreType.DMA((3,)),
            pltpu.SMEM(clip_frames.shape, jnp.int32),
            pltpu.SemaphoreType.DMA((1,)),
            pltpu.SemaphoreType.DMA((own_heads, 3)),
            pltpu.SemaphoreType.DMA((own_heads, 3)),
            pltpu.SemaphoreType.DMA((own_heads,)),
            pltpu.SemaphoreType.DMA((1,)),
            pltpu.SemaphoreType.REGULAR((2, count.bit_length())),
            pltpu.SemaphoreType.REGULAR((1,)),
        ],
        compiler_params=pltpu.CompilerParams(collective_id=0, has_side_effects=True),
    )(clip_frames, queries, keys, values)


def solution(mesh):
    split_heads = mesh.shape["seq"] >= 8 and HEADS % mesh.shape["seq"] == 0
    return jax.shard_map(
        fused_body if split_heads else body,
        mesh=mesh,
        in_specs=(P("seq", "grp", None), P("seq", "grp", None), P("seq", "grp", None), P("grp")),
        out_specs=P("seq", "grp", None),
        check_vma=False,
    )
```
